32 devices in a mesh: node: 4 (over z), band: 8 (over y, x, core).
Axes of the slice: x: 2, y: 2, z: 4, core: 2. Of those that a mesh axis runs over, the one named last changes fastest.
Arguments:
- state0: float32 [2, 1024, 4, 3, 512], P(None, 'band'), may hold values from -36 to 36
- iterate: float32 [4, 2, 1024, 4, 3, 512], P('node', None, 'band'), may hold values from -37.2 to 37.2
- legendre: bfloat16 [1024, 512, 512], P('band'), may hold values from -0.25 to 0.25
- lat_weight: float32 [512], replicated, may hold values from 0.25 to 1
- coriolis: float32 [2, 512], replicated, may hold values from -1.5 to 1.5
- damping: float32 [1024, 3, 512], P('band'), may hold values from 0.1 to 10
- quadrature: float32 [4, 4], replicated, may hold values from 0.02 to 0.25
Outputs:
- updated: float32 [4, 2, 1024, 4, 3, 512], P('node', None, 'band')
- sweep_change: float32 [3], replicated
The draws below stay inside these ranges and needn't reach their ends.
All inputs are finite; a program needn't handle non-finite values.
Results may differ from the reference program's by a relative error of at most 0.0017.
Values may be sent and summed in bfloat16 or wider, within the bound.
A program may use at most 256 MiB of HBM per device.

```python
import math
import jax
import jax.numpy as jnp
from jax import lax

M = 1024
J = 512
NH = 512
ENS = 4
NLON = 2048
NODES = 4


def base_field(key):
    noise_key, row_key, col_key = jax.random.split(key, 3)
    shape = (2, M, ENS, 3, J)
    noise = jnp.clip(jax.random.normal(noise_key, shape, jnp.float32), -4.0, 4.0)
    low = math.log(0.3)
    high = math.log(3.0)
    rows = jnp.exp(jax.random.uniform(row_key, (1, M, 1, 3, 1), jnp.float32, low, high))
    cols = jnp.exp(jax.random.uniform(col_key, (1, 1, 1, 1, J), jnp.float32, low, high))
    return noise * rows * cols


def draw_state0(key, part):
    return base_field(jax.random.fold_in(key, 11)).astype(jnp.float32)


def draw_iterate(key, part):
    start = base_field(jax.random.fold_in(key, 11))
    noise = jnp.clip(jax.random.normal(jax.random.fold_in(key, 12), (NODES,) + start.shape, jnp.float32), -4.0, 4.0)
    return (start[None] + 0.3 * noise).astype(jnp.float32)


def levels(key, extent, cuts, smallest, high):
    loudness = 1.0
    for position, blocks in cuts:
        heights = jax.random.uniform(jax.random.fold_in(jax.random.fold_in(key, 6), position), (blocks,), jnp.float32, smallest / len(cuts), high / len(cuts))
        loudness = loudness * jnp.repeat(jnp.exp(heights), extent[position] // blocks).reshape((-1,) + (1,) * (len(extent) - 1 - position))
    return loudness


def gaussian(key, extent, spread, limit, cuts=(), kind=jnp.bfloat16):
    gain = levels(key, extent, cuts, -0.22, 0.18) if cuts else 1.0
    drawn = jax.random.normal(key, extent, jnp.float32) * spread * gain
    return jnp.minimum(jnp.maximum(drawn, -limit), limit).astype(kind)


def setup_inputs(seed: int = 0) -> dict:
    keys = jax.random.split(jax.random.key(seed), 8)
    return {
        "state0": draw_state0(jax.random.fold_in(keys[7], 71), 0),
        "iterate": draw_iterate(jax.random.fold_in(keys[7], 71), 0),
        "legendre": gaussian(keys[2], (M, NH, J), J ** -0.5, 0.25, ((0, 8),)),
        "lat_weight": jnp.clip(jax.random.uniform(keys[3], (NH,), jnp.float32, 0.25, 1.0), 0.25, 1.0),
        "coriolis": jnp.clip(jax.random.uniform(keys[4], (2, NH), jnp.float32, -1.5, 1.5), -1.5, 1.5),
        "damping": jnp.clip(jnp.exp(math.log(10.0) - 4.6051702 * jax.random.uniform(keys[5], (M, 3, J), jnp.float32) ** levels(keys[5], (M, 3, J), ((0, 8),), -0.2, 0.2)), 0.1, 10.0),
        "quadrature": jnp.clip(jax.random.uniform(keys[6], (NODES, NODES), jnp.float32, 0.02, 0.25), 0.02, 0.25),
    }


def to_grid(coeffs):
    first = (2.0 * jnp.real(coeffs[..., :1])).astype(coeffs.dtype)
    tail = jnp.zeros(coeffs.shape[:-1] + (NLON // 2 + 1 - M,), coeffs.dtype)
    padded = jnp.concatenate([first, coeffs[..., 1:], tail], axis=-1)
    return math.sqrt(M) * jnp.fft.irfft(padded, n=NLON, axis=-1)

def node_force(spec, legendre, lat_weight, coriolis, damping):
    half = J // 2
    table = legendre.astype(jnp.float32)
    coeff = spec.astype(jnp.bfloat16).astype(jnp.float32)
    even = jnp.einsum('cmefj,mlj->cmefl', coeff[..., :half], table[:, :, :half])
    odd = jnp.einsum('cmefj,mlj->cmefl', coeff[..., half:], table[:, :, half:])
    four = jnp.stack([even + odd, even - odd], axis=4)
    four = jnp.transpose(four, (0, 2, 3, 4, 5, 1))
    comp = four[0] + 1j * four[1]
    wave = jnp.arange(M, dtype=jnp.float32) / M
    values = to_grid(comp)
    slopes = to_grid(1j * wave * comp)
    u_wind, v_wind, height = (values[:, 0], values[:, 1], values[:, 2])
    u_slope, v_slope, h_slope = (slopes[:, 0], slopes[:, 1], slopes[:, 2])
    cor = coriolis[:, :, None]
    tend_u = -u_wind * u_slope + cor * v_wind - h_slope
    tend_v = -u_wind * v_slope - cor * u_wind
    tend_h = -u_wind * h_slope - (1.0 + height) * u_slope
    tend = jnp.stack([tend_u, tend_v, tend_h], axis=1)
    spectrum = jnp.fft.rfft(tend, axis=-1)[..., :M] / math.sqrt(M)
    weight = lat_weight[:, None]
    sym = weight * (spectrum[:, :, 0] + spectrum[:, :, 1])
    anti = weight * (spectrum[:, :, 0] - spectrum[:, :, 1])

    def to_real(z):
        parts = jnp.stack([jnp.real(z), jnp.imag(z)], axis=0)
        parts = jnp.transpose(parts, (0, 4, 1, 2, 3))
        return parts.astype(jnp.bfloat16).astype(jnp.float32)
    sym_r = to_real(sym)
    anti_r = to_real(anti)
    spec_even = jnp.einsum('cmefl,mlj->cmefj', sym_r, table[:, :, :half])
    spec_odd = jnp.einsum('cmefl,mlj->cmefj', anti_r, table[:, :, half:])
    nonlinear = jnp.concatenate([spec_even, spec_odd], axis=-1)
    return nonlinear - damping[None, :, None] * spec

def reference(state0, iterate, legendre, lat_weight, coriolis, damping, quadrature):
    force = lax.map(lambda spec: node_force(spec, legendre, lat_weight, coriolis, damping), iterate)
    mixed = jnp.tensordot(quadrature, force, axes=1, precision=lax.Precision.HIGHEST)
    diag = jnp.diagonal(quadrature)[:, None, None, None, None, None]
    rate = damping[None, None, :, None, :, :]
    updated = (state0[None] + mixed + diag * rate * iterate) / (1.0 + diag * rate)
    change = lax.optimization_barrier(jnp.sum((updated - iterate) ** 2, axis=(0, 1, 2, 3, 5)))
    base = lax.optimization_barrier(jnp.sum(state0 ** 2, axis=(0, 1, 2, 4)))
    sweep_change = jnp.sqrt(change / (NODES * base + 1e-06))
    return (updated, sweep_change)
```

```python
import math

import jax
import jax.numpy as jnp
from jax import lax
from jax.sharding import PartitionSpec as P


def split_bf16(x):
    high = lax.reduce_precision(x, 8, 7)
    return high.astype(jnp.bfloat16), (x - high).astype(jnp.bfloat16)


def dft_table(parity, nband, local_modes, modes, points):
    fine = 32
    coarse = modes // fine
    column = lax.iota(jnp.int32, modes)
    pairs = local_modes // 2
    part = column // pairs % 2
    wave = column // local_modes * local_modes + column % pairs * 2 + parity
    unit = 2.0 * math.pi / points

    def angle(index):
        return (index % points).astype(jnp.float32) * unit

    big = angle(
        lax.iota(jnp.int32, coarse)[:, None] * fine * wave[None] + part[None] * (points // 4)
    )
    small = angle(lax.iota(jnp.int32, fine)[:, None] * wave[None])
    cos_big, sin_big = jnp.cos(big)[:, None], jnp.sin(big)[:, None]
    cos_small, sin_small = jnp.cos(small)[None], jnp.sin(small)[None]
    scale = 1.0 / math.sqrt(modes)
    slope_scale = wave.astype(jnp.float32) * (scale / modes)
    value = (cos_big * cos_small - sin_big * sin_small).reshape(modes, modes) * scale
    slope = -(sin_big * cos_small + cos_big * sin_small).reshape(modes, modes) * slope_scale
    return split_bf16(value), split_bf16(slope)


def mul(a, b, dims):
    return lax.dot_general(a, b, (dims, ((), ())), preferred_element_type=jnp.float32)


def body(state0, iterate, legendre, lat_weight, coriolis, damping, quadrature):
    spec = iterate[0]
    degrees = legendre.shape[2]
    half = degrees // 2
    local_modes, hemi = legendre.shape[:2]
    members, fields = spec.shape[2:4]
    nband = lax.axis_size("band")
    nnode = lax.axis_size("node")
    modes = local_modes * nband
    points = 2 * modes
    pairs = local_modes // 2
    lat_rows = hemi // nband
    node = lax.axis_index("node")
    band = lax.axis_index("band")
    tables = [dft_table(p, nband, local_modes, modes, points) for p in range(2)]
    cor = lax.dynamic_slice_in_dim(coriolis, band * lat_rows, lat_rows, 1)
    weight = lax.dynamic_slice_in_dim(lat_weight, band * lat_rows, lat_rows, 0)
    quad_row = lax.dynamic_slice_in_dim(quadrature, node, 1, 0)[0]
    diag = lax.dynamic_slice(quadrature, (node, node), (1, 1))[0, 0]
    is_even = lax.iota(jnp.int32, degrees) < half
    rate = damping[None, :, None]

    groups = 2
    ens = members // groups

    def synthesis(first):
        coeff = spec[:, :, first : first + ens].astype(jnp.bfloat16)
        coeff = coeff.transpose(1, 0, 3, 2, 4)
        zero = jnp.zeros((), jnp.bfloat16)
        rows = jnp.stack([jnp.where(is_even, coeff, zero), jnp.where(is_even, zero, coeff)], axis=1)
        rows = rows.reshape(local_modes, 4 * fields * ens, degrees)
        four = jnp.einsum("mrj,mlj->mrl", rows, legendre, preferred_element_type=jnp.float32)
        four = four.astype(jnp.bfloat16)
        four = four.reshape(pairs, 2, 2, 2, fields, ens, nband, lat_rows)
        four = four.transpose(6, 1, 3, 0, 2, 4, 5, 7)
        four = four.reshape(nband, 2, 2, pairs, 2 * fields * ens * lat_rows)
        return lax.all_to_all(four, "band", split_axis=0, concat_axis=0, tiled=True)

    def grid_step(four):
        shape = (modes, 2, fields, ens * lat_rows)
        parts = []
        for p in range(2):
            x = four[:, p].reshape(modes, -1)
            pair = []
            for high, low in tables[p]:
                dims = ((1,), (0,))
                pair.append((mul(high, x, dims) + mul(low, x, dims)).reshape(shape))
            parts.append(pair)
        tends = []
        for h in range(2):
            value, slope = (
                parts[0][v] + parts[1][v] if h == 0 else parts[0][v] - parts[1][v] for v in range(2)
            )
            hemis = []
            for s in range(2):
                val, slo = (
                    g[:, 0] + g[:, 1] if s == 0 else g[:, 0] - g[:, 1] for g in (value, slope)
                )
                c = jnp.tile(cor[s], ens)
                u, v, z = (val[:, f] for f in range(3))
                du, dv, dz = (slo[:, f] for f in range(3))
                hemis.append(
                    jnp.stack(
                        [-u * du + c * v - dz, -u * dv - c * u, -u * dz - (1.0 + z) * du], axis=1
                    )
                )
            tends.append(jnp.stack([hemis[0] + hemis[1], hemis[0] - hemis[1]], axis=1))
        scale = jnp.tile(weight, 2 * fields * ens)
        spectra = []
        for p in range(2):
            z = tends[0] + tends[1] if p == 0 else tends[0] - tends[1]
            zh, zl = split_bf16(z.reshape(modes, -1))
            high, low = tables[p][0]
            dims = ((0,), (0,))
            s = mul(high, zh, dims) + mul(high, zl, dims) + mul(low, zh, dims)
            spectra.append((s * scale).astype(jnp.bfloat16).reshape(nband, 2, pairs, -1))
        out = jnp.stack(spectra, axis=1)
        return lax.all_to_all(out, "band", split_axis=0, concat_axis=0, tiled=True)

    def analysis(out, first):
        out = out.reshape(nband, 2, 2, pairs, 2, fields, ens, lat_rows)
        out = out.transpose(3, 1, 4, 2, 5, 6, 0, 7)
        out = out.reshape(local_modes, 4 * fields * ens, hemi)
        both = jnp.einsum("mrl,mlj->mrj", out, legendre, preferred_element_type=jnp.float32)
        both = both.reshape(local_modes, 2, 2, fields, ens, degrees)
        nonlinear = jnp.where(is_even, both[:, 0], both[:, 1]).transpose(1, 0, 3, 2, 4)
        part = slice(first, first + ens)
        rest = nonlinear - rate * (spec[:, :, part] - state0[:, :, part])
        gathered = lax.all_gather(rest.astype(jnp.bfloat16), "node")
        mixed = sum(quad_row[p] * gathered[p].astype(jnp.float32) for p in range(nnode))
        return mixed

    received = [synthesis(g * ens) for g in range(groups)]
    spectra = [grid_step(r) for r in received]
    mixed = [analysis(s, g * ens) for g, s in enumerate(spectra)]
    mixed = jnp.concatenate(mixed, axis=2) - jnp.sum(quad_row) * (rate * state0)
    updated = (state0 + mixed + diag * rate * spec) / (1.0 + diag * rate)
    change = jnp.sum((updated - spec) ** 2, axis=(0, 1, 2, 4))
    base = jnp.sum(state0 * state0, axis=(0, 1, 2, 4))
    total = lax.psum(jnp.stack([change, base]), ("node", "band"))
    ratio = jnp.sqrt(total[0] / (total[1] + 1e-06))
    return (updated[None], ratio)


def solution(mesh):
    placed = (
        P(None, "band", None, None, None),
        P("node", None, "band", None, None, None),
        P("band", None, None),
        P(),
        P(),
        P("band", None, None),
        P(),
    )
    return jax.shard_map(
        body,
        mesh=mesh,
        in_specs=placed,
        out_specs=(P("node", None, "band", None, None, None), P()),
        check_vma=False,
    )
```
